128 devices in a mesh: row: 16 (over z_lo, y, core), col: 8 (over z_hi, x).
Axes of the slice: x: 4, y: 4, z: 4 (z_hi: 2, z_lo: 2; z = z_hi * 2 + z_lo), core: 2. Of those that a mesh axis runs over, the one named last changes fastest.
Arguments:
- adj_tiles: bfloat16 [16, 8, 448, 128, 128], P('row', 'col'), may hold values from -0.03125 to 0.03125
- tile_counts: int32 [16, 8, 16], P('row', 'col'), may hold values from 5 to 32, as said below
- tile_cols: int32 [16, 8, 448], P('row', 'col'), may hold values from 0 to 31, as said below
- features: bfloat16 [32768, 256], P(('col', 'row')), may hold values from -6 to 6
- weight: bfloat16 [256, 256], replicated, may hold values from -0.375 to 0.375
- upstream: bfloat16 [32768, 256], P(('row', 'col')), may hold values from -6 to 6
Outputs:
- hidden: bfloat16 [32768, 256], P(('row', 'col'))
- weight_grad: float32 [256, 256], replicated
- feature_grad: bfloat16 [32768, 256], P(('col', 'row'))
The draws below stay inside these ranges and needn't reach their ends.
Inputs may be any that keep to these rules, and one draw needn't show every extreme that they name: `tile_counts`: entry (r, c, t) counts the nonzero tiles of row tile t in block (r, c); the counts of one block sum to 448 or less, and to exactly 448 in at least one block. `tile_cols`: live slots are filled in order of row tile; the entries of slots past a block's total count are not used.
All inputs are finite; a program needn't handle non-finite values.
Results may differ from the reference program's by a relative error of at most 0.023.
Values may be sent and summed in bfloat16 or wider, within the bound.
A program may use at most 128 MiB of HBM per device.

```python
import jax
import jax.numpy as jnp
from jax import lax

F = 256
TILE = 128
RT = 16
FILL_ROW = 28
CT = 32
SLOTS = 448
NODES = 32768
N_ROW = 16
N_COL = 8


def pattern(key):
    base_key = jax.random.fold_in(key, 7013)
    key_full, key_high, key_drop, key_shift, key_start, key_stride = jax.random.split(base_key, 6)
    devices_all = N_ROW * N_COL
    spread = min(4, CT - FILL_ROW, FILL_ROW)
    lowest = max(1, FILL_ROW // 3)
    full_dev = jax.random.randint(key_full, (), 0, devices_all)
    highs = jax.random.randint(key_high, (devices_all, 1), lowest, FILL_ROW + 1)
    drops = jax.random.randint(key_drop, (devices_all, RT), 0, 1 << 20) % (highs // 2 + 1)
    drawn = highs - drops
    half_rows = RT // 2
    shifts = jax.random.randint(key_shift, (half_rows,), -spread, spread + 1)
    shifts = shifts.at[0].set(spread)
    fulls = FILL_ROW + jnp.concatenate([shifts, -shifts])
    is_full = (jnp.arange(devices_all, dtype=jnp.int32) == full_dev)[:, None]
    counts = jnp.where(is_full, fulls[None, :], drawn).astype(jnp.int32)
    ending = jnp.cumsum(counts, axis=1).astype(jnp.int32)
    starts = ending - counts
    position = jnp.arange(SLOTS, dtype=jnp.int32)
    row_of = jnp.sum((position[None, :, None] >= ending[:, None, :]).astype(jnp.int32), axis=2)
    clipped = jnp.minimum(row_of, RT - 1)
    within = position[None, :] - jnp.take_along_axis(starts, clipped, axis=1)
    offsets = jax.random.randint(key_start, (devices_all, RT), 0, CT)
    strides = 2 * jax.random.randint(key_stride, (devices_all, RT), 0, max(1, CT // 2)) + 1
    slot_off = jnp.take_along_axis(offsets, clipped, axis=1)
    slot_stride = jnp.take_along_axis(strides, clipped, axis=1)
    live = row_of < RT
    col_ids = jnp.where(live, (slot_off + within * slot_stride) % CT, position[None, :] % CT)
    return (counts.reshape(N_ROW, N_COL, RT), col_ids.astype(jnp.int32).reshape(N_ROW, N_COL, SLOTS))


def draw_tile_counts(key, part):
    counts, col_ids = pattern(key)
    return counts


def draw_tile_cols(key, part):
    counts, col_ids = pattern(key)
    return col_ids


def block_scale(stream_key, shape, cuts, smallest, high):
    loudness, own = 1.0, jax.random.fold_in(stream_key, 6)
    for dim, blocks in cuts:
        steps = jnp.exp(jax.random.uniform(jax.random.fold_in(own, dim), (blocks,), jnp.float32, smallest / len(cuts), high / len(cuts)))
        loudness = loudness * jnp.repeat(steps, shape[dim] // blocks).reshape([-1 if axis == dim else 1 for axis in range(len(shape))])
    return loudness


def centred(own_key, shape, scale, bound, shards=(), kind=jnp.bfloat16):
    factor_of = block_scale(own_key, shape, shards, -0.22, 0.18) if shards else 1.0
    array = jax.random.normal(own_key, shape, jnp.float32) * scale * factor_of
    return jnp.minimum(jnp.maximum(array, -bound), bound).astype(kind)


def setup_inputs(seed: int = 0) -> dict:
    seeds = jax.random.split(jax.random.key(seed), 7)
    return {
        "adj_tiles": centred(seeds[0], (N_ROW, N_COL, SLOTS, TILE, TILE), (FILL_ROW * N_COL * TILE) ** -0.5, 0.03125, ((0, 16), (1, 8))),
        "tile_counts": draw_tile_counts(jax.random.fold_in(seeds[6], 71), 0),
        "tile_cols": draw_tile_cols(jax.random.fold_in(seeds[6], 71), 0),
        "features": centred(seeds[3], (NODES, F), 1.0, 6.0, ((0, 128),)),
        "weight": centred(seeds[4], (F, F), F ** -0.5, 0.375),
        "upstream": centred(seeds[5], (NODES, F), 1.0, 6.0, ((0, 128),)),
    }


def membership(counts, slots):
    ending = jnp.cumsum(counts).astype(jnp.int32)
    starts = ending - counts
    position = jnp.arange(slots, dtype=jnp.int32)[:, None]
    return ((position >= starts[None, :]) & (position < ending[None, :])).astype(jnp.float32)

def forward_block(adj_block, col_ids, counts, col_block):
    rows_t = counts.shape[0]
    group_size = adj_block.shape[0] // rows_t
    col_tiles = col_block.shape[0] // TILE
    member = membership(counts, adj_block.shape[0])
    block_tiles = col_block.reshape(col_tiles, TILE, F)

    def advance(total, pieces):
        tile_g, col_g, mem_g = pieces
        picked = block_tiles[col_g].astype(jnp.float32)
        product = jnp.einsum('sij,sjf->sif', tile_g.astype(jnp.float32), picked, precision=lax.Precision.HIGHEST)
        return (total + jnp.einsum('st,sif->tif', mem_g, product, precision=lax.Precision.HIGHEST), None)
    stacked = (adj_block.reshape(rows_t, group_size, TILE, TILE), col_ids.reshape(rows_t, group_size), member.reshape(rows_t, group_size, rows_t))
    total, unused = lax.scan(advance, jnp.zeros((rows_t, TILE, F), jnp.float32), stacked)
    return total.reshape(rows_t * TILE, F)

def backward_block(adj_block, col_ids, counts, row_grad, col_tiles):
    rows_t = counts.shape[0]
    group_size = adj_block.shape[0] // rows_t
    member = membership(counts, adj_block.shape[0])
    grad_tiles = row_grad.reshape(rows_t, TILE, F).astype(jnp.float32)
    col_range = jnp.arange(col_tiles, dtype=jnp.int32)

    def advance(total, pieces):
        tile_g, col_g, mem_g = pieces
        chosen = jnp.einsum('st,tif->sif', mem_g, grad_tiles, precision=lax.Precision.HIGHEST)
        product = jnp.einsum('sij,sif->sjf', tile_g.astype(jnp.float32), chosen, precision=lax.Precision.HIGHEST)
        onehot = (col_g[:, None] == col_range[None, :]).astype(jnp.float32)
        return (total + jnp.einsum('sc,sjf->cjf', onehot, product, precision=lax.Precision.HIGHEST), None)
    stacked = (adj_block.reshape(rows_t, group_size, TILE, TILE), col_ids.reshape(rows_t, group_size), member.reshape(rows_t, group_size, rows_t))
    total, unused = lax.scan(advance, jnp.zeros((col_tiles, TILE, F), jnp.float32), stacked)
    return total.reshape(col_tiles * TILE, F)

def reference(adj_tiles, tile_counts, tile_cols, features, weight, upstream):
    feat_blocks = features.reshape(N_COL, CT * TILE, F)

    def row_pass(row_id):

        def col_step(total, col_id):
            part = forward_block(adj_tiles[row_id, col_id], tile_cols[row_id, col_id], tile_counts[row_id, col_id], feat_blocks[col_id])
            return (total + part, None)
        total, unused = lax.scan(col_step, jnp.zeros((RT * TILE, F), jnp.float32), jnp.arange(N_COL, dtype=jnp.int32))
        return total
    partial_value = lax.map(row_pass, jnp.arange(N_ROW, dtype=jnp.int32))
    aggregated = partial_value.reshape(NODES, F).astype(jnp.bfloat16)
    pre = jnp.dot(aggregated, weight, preferred_element_type=jnp.float32)
    hidden = jax.nn.silu(pre).astype(jnp.bfloat16)
    sigmoid_pre = jax.nn.sigmoid(pre)
    pre_grad = (upstream.astype(jnp.float32) * sigmoid_pre * (1.0 + pre * (1.0 - sigmoid_pre))).astype(jnp.bfloat16)
    weight_grad = jnp.dot(aggregated.T, pre_grad, preferred_element_type=jnp.float32) / jnp.sqrt(jnp.float32(NODES))
    agg_grad = jnp.dot(pre_grad, weight.T, preferred_element_type=jnp.float32).astype(jnp.bfloat16)
    grad_blocks = agg_grad.reshape(N_ROW, RT * TILE, F)

    def col_pass(col_id):

        def row_step(total, row_id):
            part = backward_block(adj_tiles[row_id, col_id], tile_cols[row_id, col_id], tile_counts[row_id, col_id], grad_blocks[row_id], CT)
            return (total + part, None)
        total, unused = lax.scan(row_step, jnp.zeros((CT * TILE, F), jnp.float32), jnp.arange(N_ROW, dtype=jnp.int32))
        return total
    columns = lax.map(col_pass, jnp.arange(N_COL, dtype=jnp.int32))
    feature_grad = columns.reshape(NODES, F).astype(jnp.bfloat16)
    return (hidden, weight_grad, feature_grad)
```

```python
import functools
import math

import jax
import jax.numpy as jnp
from jax import lax
from jax.experimental import pallas as pl
from jax.experimental.pallas import tpu as pltpu
from jax.sharding import PartitionSpec as P

MESH = pl.DeviceIdType.MESH
F32, BF16 = jnp.float32, jnp.bfloat16


def slot_tables(counts, cols, col_tiles):
    slots, rows_t = cols.shape[0], counts.shape[0]
    tiles = jnp.arange(rows_t, dtype=jnp.int32)
    ending = jnp.sum(jnp.where(tiles[None, :] <= tiles[:, None], counts[None, :], 0), axis=1)
    position = jnp.arange(slots, dtype=jnp.int32)
    row = jnp.sum((position[:, None] >= ending[None, :]).astype(jnp.int32), axis=1)
    key = jnp.where(row < rows_t, row * col_tiles + cols, -1 - position)
    places = jnp.arange(rows_t * col_tiles, dtype=jnp.int32)
    slot_of = jnp.min(jnp.where(key[None, :] == places[:, None], position[None, :], slots), axis=1)
    later = (key[None, :] == key[:, None]) & (position[None, :] > position[:, None])
    next_of = jnp.min(jnp.where(later, position[None, :], slots), axis=1)
    return slot_of, next_of


def layer_kernel(
    n_row, n_col, scale,
    slot_of, next_of, adj, feat, weight, upstream,
    hidden, weight_grad, feature_grad,
    a_v, x_v, send2, recv2, d_v, send_p, recv_p, acc4, send4, recv4, wl, w1, w2, w3,
    adj_sem, x_send, x_recv, xr_send, xr_recv, s2_send, s2_recv, d_send, d_recv,
    p_send, p_recv, s4_send, s4_recv, w1_send, w1_recv, w2_send, w2_recv, w3_send, w3_recv,
):
    slots = adj.shape[0]
    tile = adj.shape[1]
    piece = feat.shape[0]
    width = feat.shape[1]
    chips = n_row // 2
    col_tiles = (piece * n_row) // tile
    row = lax.axis_index("row")
    col = lax.axis_index("col")
    chip, core = row // 2, row % 2
    partner = row + 1 - 2 * core
    half_r, half_c = chips // 2, n_col // 2
    cy, cz = chip % half_r, chip // half_r
    kx, kz = col % half_c, col // half_c

    def chip_at(i):
        return ((cz + i // half_r) % 2) * half_r + (cy + i) % half_r

    def col_at(i):
        return ((kz + i // half_c) % 2) * half_c + (kx + i) % half_c

    def chip_from(i):
        return ((cz + i // half_r) % 2) * half_r + (cy + half_r - i % half_r) % half_r

    def col_from(i):
        return ((kz + i // half_c) % 2) * half_c + (kx + half_c - i % half_c) % half_c

    def rows_of(ref, r):
        return ref.at[pl.ds(pl.multiple_of(r * piece, piece), piece)]

    def remote(src, dst, send, recv, r, c):
        return pltpu.make_async_remote_copy(
            src_ref=src, dst_ref=dst, send_sem=send, recv_sem=recv, device_id=(r, c), device_id_type=MESH
        )

    adj_copy = pltpu.make_async_copy(adj, a_v.at[pl.ds(0, slots)], adj_sem)
    adj_copy.start()
    a_v[slots] = jnp.zeros((tile, tile), BF16)

    barrier = pltpu.get_barrier_semaphore()
    for i in range(1, n_row):
        pl.semaphore_signal(barrier, inc=1, device_id=((row + i) % n_row, col), device_id_type=MESH)
    for i in range(1, n_col):
        pl.semaphore_signal(barrier, inc=1, device_id=(row, (col + i) % n_col), device_id_type=MESH)
    pl.semaphore_wait(barrier, n_row + n_col - 2)

    def x_copy(i):
        return remote(feat, rows_of(x_v, row), x_send.at[i], x_recv.at[i], 2 * chip_at(i) + core, col)

    def x_relay(i, source):
        r = 2 * chip_from(i) + core
        return remote(source, rows_of(x_v, r), xr_send.at[i], xr_recv.at[i], partner, col)

    x_order = [i for i in range(1, chips)]
    for i in x_order:
        x_copy(i).start()
    x_relay(0, feat).start()
    x_v[pl.ds(pl.multiple_of(row * piece, piece), piece), :] = feat[...]

    adj_copy.wait()

    def merge(k, carry):
        s = slots - 1 - k
        a_v[s] = a_v[s] + a_v[next_of[s]]
        return carry

    lax.fori_loop(0, slots, merge, 0)

    for i in x_order:
        x_copy(i).wait_recv()
        x_relay(i, rows_of(x_v, 2 * chip_from(i) + core)).start()
    for i in range(chips):
        x_relay(i, feat).wait_recv()

    def forward(dest):
        parts = []
        for t in range(piece // tile):
            base = (dest * (piece // tile) + t) * col_tiles
            parts.append(jnp.concatenate([a_v[slot_of[base + k]] for k in range(col_tiles)], axis=1))
        return jnp.dot(jnp.concatenate(parts, axis=0), x_v[...], preferred_element_type=F32)

    def s2_copy(i):
        return remote(send2.at[i], recv2.at[i], s2_send.at[i], s2_recv.at[i], row, col_at(i))

    def forward_step(k, carry):
        i = k + 1
        send2[i] = forward(col_at(i)).astype(BF16)
        s2_copy(i).start()
        return carry

    lax.fori_loop(0, n_col - 1, forward_step, 0)
    total = forward(col)
    for i in range(1, n_col):
        s2_copy(i).wait_recv()
        total = total + recv2[i].astype(F32)
    aggregated = total.astype(BF16)

    pre = jnp.dot(aggregated, weight[...], preferred_element_type=F32)
    gate = jax.nn.sigmoid(pre)
    hidden[...] = (pre * gate).astype(BF16)
    pre_grad = (upstream[...].astype(F32) * gate * (1.0 + pre * (1.0 - gate))).astype(BF16)
    grad_t = lax.dot_general(weight[...], pre_grad, (((1,), (1,)), ((), ())), preferred_element_type=F32)
    d_v[col] = grad_t.astype(BF16)

    def d_copy(i):
        return remote(d_v.at[col], d_v.at[col], d_send.at[i], d_recv.at[i], row, col_at(i))

    for i in range(1, n_col):
        d_copy(i).start()

    agg_t = jnp.transpose(aggregated.astype(F32)).astype(BF16)
    wl[...] = jnp.dot(agg_t, pre_grad, preferred_element_type=F32).reshape(wl.shape)

    def w1_copy(i):
        r = (row + i) % n_row
        return remote(wl.at[r], w1.at[i], w1_send.at[i], w1_recv.at[i], r, col)

    def w2_copy(i):
        return remote(w2.at[col], w2.at[col], w2_send.at[i], w2_recv.at[i], row, col_at(i))

    def w3_copy(i):
        return remote(w3.at[row], w3.at[row], w3_send.at[i], w3_recv.at[i], (row + i) % n_row, col)

    for i in range(1, n_row):
        w1_copy(i).start()
    slice_sum = wl[row]
    for i in range(1, n_row):
        w1_copy(i).wait_recv()
        slice_sum = slice_sum + w1[i]
    w2[col] = slice_sum
    for i in range(1, n_col):
        w2_copy(i).start()
    for i in range(1, n_col):
        d_copy(i).wait_recv()
    for i in range(1, n_col):
        w2_copy(i).wait_recv()
    slice_sum = w2[0]
    for c in range(1, n_col):
        slice_sum = slice_sum + w2[c]
    w3[row] = slice_sum * scale
    for i in range(1, n_row):
        w3_copy(i).start()

    def backward(dest):
        acc = None
        for c in range(n_col):
            lines = []
            for t in range(piece // tile):
                base = (c * (piece // tile) + t) * col_tiles + dest * (piece // tile)
                lines.append(jnp.concatenate([a_v[slot_of[base + k]] for k in range(piece // tile)], axis=1))
            part = jnp.dot(d_v[c], jnp.concatenate(lines, axis=0), preferred_element_type=F32)
            acc = part if acc is None else acc + part
        return acc

    def p_copy(i):
        return remote(send_p.at[i], recv_p.at[i], p_send.at[i], p_recv.at[i], partner, col)

    def s4_copy(i):
        return remote(send4.at[i], recv4.at[i], s4_send.at[i], s4_recv.at[i], 2 * chip_at(i) + core, col)

    def backward_step(k, carry):
        i = (k + 1) % chips
        dest = chip_at(i)
        send_p[i] = backward(2 * dest + 1 - core).astype(BF16)
        p_copy(i).start()
        acc4[i] = backward(2 * dest + core)

        @pl.when(k > 0)
        def _():
            p_copy(k).wait_recv()
            send4[k] = (acc4[k] + recv_p[k].astype(F32)).astype(BF16)
            s4_copy(k).start()

        return carry

    lax.fori_loop(0, chips, backward_step, 0)
    p_copy(0).wait_recv()
    total = acc4[0] + recv_p[0].astype(F32)
    for i in range(1, n_row):
        w3_copy(i).wait_recv()
    weight_grad[...] = w3[...].reshape(weight_grad.shape)
    for i in range(1, chips):
        s4_copy(i).wait_recv()
        total = total + recv4[i].astype(F32)
    feature_grad[...] = jnp.transpose(total).astype(BF16)

    for i in range(1, chips):
        x_copy(i).wait_send()
        s4_copy(i).wait_send()
    for i in range(chips):
        x_relay(i, feat).wait_send()
        p_copy(i).wait_send()
    for i in range(1, n_col):
        s2_copy(i).wait_send()
        d_copy(i).wait_send()
        w2_copy(i).wait_send()
    for i in range(1, n_row):
        w1_copy(i).wait_send()
        w3_copy(i).wait_send()


def solution(mesh):
    n_row, n_col = mesh.shape["row"], mesh.shape["col"]
    chips = n_row // 2

    def shards(adj_tiles, tile_counts, tile_cols, features, weight, upstream):
        adj = adj_tiles[0, 0]
        slots, tile = adj.shape[0], adj.shape[1]
        piece, width = features.shape
        nodes = piece * n_row * n_col
        slot_of, next_of = slot_tables(tile_counts[0, 0], tile_cols[0, 0], piece * n_row // tile)
        sl = width // n_row
        dma = pltpu.SemaphoreType.DMA
        vmem = pl.BlockSpec(memory_space=pltpu.VMEM)
        smem = pl.BlockSpec(memory_space=pltpu.SMEM)
        return pl.pallas_call(
            functools.partial(layer_kernel, n_row, n_col, 1.0 / math.sqrt(nodes)),
            out_shape=(
                jax.ShapeDtypeStruct((piece, width), BF16),
                jax.ShapeDtypeStruct((width, width), F32),
                jax.ShapeDtypeStruct((piece, width), BF16),
            ),
            in_specs=[smem, smem, pl.BlockSpec(memory_space=pl.ANY), vmem, vmem, vmem],
            out_specs=(vmem, vmem, vmem),
            scratch_shapes=[
                pltpu.VMEM((slots + 1, tile, tile), BF16),
                pltpu.VMEM((piece * n_row, width), BF16),
                pltpu.VMEM((n_col, piece, width), BF16),
                pltpu.VMEM((n_col, piece, width), BF16),
                pltpu.VMEM((n_col, width, piece), BF16),
                pltpu.VMEM((chips, width, piece), BF16),
                pltpu.VMEM((chips, width, piece), BF16),
                pltpu.VMEM((chips, width, piece), F32),
                pltpu.VMEM((chips, width, piece), BF16),
                pltpu.VMEM((chips, width, piece), BF16),
                pltpu.VMEM((n_row, sl, width), F32),
                pltpu.VMEM((n_row, sl, width), F32),
                pltpu.VMEM((n_col, sl, width), F32),
                pltpu.VMEM((n_row, sl, width), F32),
                dma,
                dma((chips,)), dma((chips,)), dma((chips,)), dma((chips,)),
                dma((n_col,)), dma((n_col,)), dma((n_col,)), dma((n_col,)),
                dma((chips,)), dma((chips,)), dma((chips,)), dma((chips,)),
                dma((n_row,)), dma((n_row,)), dma((n_col,)), dma((n_col,)),
                dma((n_row,)), dma((n_row,)),
            ],
            compiler_params=pltpu.CompilerParams(
                collective_id=0, has_side_effects=True, vmem_limit_bytes=56 * 1024 * 1024
            ),
        )(slot_of, next_of, adj, features, weight, upstream)

    return jax.shard_map(
        shards,
        mesh=mesh,
        in_specs=(
            P("row", "col", None, None, None),
            P("row", "col", None),
            P("row", "col", None),
            P(("col", "row"), None),
            P(),
            P(("row", "col"), None),
        ),
        out_specs=(P(("row", "col"), None), P(), P(("col", "row"), None)),
        check_vma=False,
    )
```

```python
import functools
import math

import jax
import jax.numpy as jnp
from jax import lax
from jax.experimental import pallas as pl
from jax.experimental.pallas import tpu as pltpu
from jax.sharding import PartitionSpec as P

MESH = pl.DeviceIdType.MESH
F32, BF16 = jnp.float32, jnp.bfloat16
ADJ_CHUNKS = 8
ADJ_FIRST = 0


def slot_tables(counts, cols, col_tiles):
    slots, rows_t = cols.shape[0], counts.shape[0]
    tiles = jnp.arange(rows_t, dtype=jnp.int32)
    ending = jnp.sum(jnp.where(tiles[None, :] <= tiles[:, None], counts[None, :], 0), axis=1)
    position = jnp.arange(slots, dtype=jnp.int32)
    row = jnp.sum((position[:, None] >= ending[None, :]).astype(jnp.int32), axis=1)
    key = jnp.where(row < rows_t, row * col_tiles + cols, -1 - position)
    places = jnp.arange(rows_t * col_tiles, dtype=jnp.int32)
    slot_of = jnp.min(jnp.where(key[None, :] == places[:, None], position[None, :], slots), axis=1)
    later = (key[None, :] == key[:, None]) & (position[None, :] > position[:, None])
    next_of = jnp.min(jnp.where(later, position[None, :], slots), axis=1)
    return slot_of, next_of


def copy_kernel(*refs):
    for source, target in zip(refs[: len(refs) // 2], refs[len(refs) // 2 :]):
        target[...] = source[...]


def layer_kernel(
    n_row, n_col, scale,
    slot_of, next_of, adj, feat, weight, upstream,
    hidden, weight_grad, feature_grad,
    a_v, x_v, d_v, acc2, acc4, send2, recv2, send4, recv4, send_p, recv_p, wl, w1, w2, w3,
    adj_sem, x_send, x_recv, xr_send, xr_recv, d_send, d_recv, s2_send, s2_recv, s4_send, s4_recv,
    p_send, p_recv, w1_send, w1_recv, w2_send, w2_recv, w3_send, w3_recv,
):
    slots, tile = adj.shape[0], adj.shape[1]
    piece = feat.shape[0]
    per = piece // tile
    chips = n_row // 2
    col_tiles = per * n_row
    row = lax.axis_index("row")
    col = lax.axis_index("col")
    chip, core = row // 2, row % 2
    partner = row + 1 - 2 * core
    half_r, half_c = chips // 2, n_col // 2

    def chip_at(i):
        return ((chip // half_r + i // half_r) % 2) * half_r + (chip % half_r + i) % half_r

    def col_at(i):
        return ((col // half_c + i // half_c) % 2) * half_c + (col % half_c + i) % half_c

    def row_device(i):
        return 2 * chip_at(i) + core, col

    def col_device(i):
        return row, col_at(i)

    def remote(src, dst, send, recv, device):
        return pltpu.make_async_remote_copy(
            src_ref=src, dst_ref=dst, send_sem=send, recv_sem=recv, device_id=device, device_id_type=MESH
        )

    def gather(piece_at, device_at, half, send, recv, hook):
        moves = (
            (0, 1), (0, half - 1), (0, half),
            (0, 2),
            (half, 1), (half, half - 1),
            (2, half),
        )

        def make(h):
            up, down, plane, two, plane_up, plane_down, plane_two = [
                remote(piece_at(p, h), piece_at(p, h), send.at[7 * h + k], recv.at[7 * h + k], device_at(to))
                for k, (p, to) in enumerate(moves)
            ]

            def step(k):
                if k == 0:
                    two.start()
                    plane.start()
                    up.start()
                    down.start()
                elif k == 1:
                    up.wait_recv()
                    hook(half - 1, h)
                    down.wait_recv()
                    hook(1, h)
                elif k == 2:
                    plane.wait_recv()
                    plane_up.start()
                    plane_down.start()
                    hook(half, h)
                elif k == 3:
                    two.wait_recv()
                    plane_two.start()
                    hook(2, h)
                else:
                    plane_up.wait_recv()
                    hook(2 * half - 1, h)
                    plane_down.wait_recv()
                    hook(half + 1, h)
                    plane_two.wait_recv()
                    hook(half + 2, h)

            def finish():
                for copy in (up, down, plane, two, plane_up, plane_down, plane_two):
                    copy.wait_send()

            return step, finish

        (step0, finish0), (step1, finish1) = make(0), make(1)
        return step0, step1, lambda: (finish0(), finish1())

    def scatter(value_at, device_at, half, send_buf, recv_buf, send, recv):
        targets = (half, 1, half - 1, 1, half - 1, 2, half)
        offsets = (half + 2, half + 1, 2 * half - 1, 1, half - 1, 2, half, 0)

        def copy_of(k, h):
            n = 7 * h + k
            return remote(send_buf.at[n], recv_buf.at[n], send.at[n], recv.at[n], device_at(targets[k]))

        def got(k, h):
            copy_of(k, h).wait_recv()
            return recv_buf[7 * h + k].astype(F32)

        before = {5: (0,), 6: (1, 2), 7: (3, 4, 6, 5)}

        def step(k, h):
            value = value_at(offsets[k], h)
            for j in before.get(k, ()):
                value = value + got(j, h)
            if k < 7:
                send_buf[7 * h + k] = value.astype(BF16)
                copy_of(k, h).start()
            return value

        def finish():
            for h in range(2):
                for k in range(7):
                    copy_of(k, h).wait_send()

        return step, finish

    def packed(numbers):
        return sum(number * 8**k for k, number in enumerate(numbers))

    first_steps = ((0, 0), (1, 0), (2, 0), (3, 0), (4, 0), (0, 1), (1, 1), (2, 1))
    second_steps = ((5, 0), (6, 0), (3, 1), (4, 1), (5, 1), (6, 1), (7, 0), (7, 1))

    def run_steps(steps, half, compute, after):
        def body(n, codes):
            code, halves = codes
            compute(code % 8, halves % 8)
            for at, act in after.items():
                pl.when(n == at)(act)
            return code // 8, halves // 8

        offsets = (half + 2, half + 1, 2 * half - 1, 1, half - 1, 2, half, 0)
        lax.fori_loop(0, 8, body, (packed(offsets[k] for k, h in steps), packed(h for k, h in steps)))

    chunk = slots // ADJ_CHUNKS

    def adj_copy(k):
        part = pl.ds(k * chunk, chunk)
        return pltpu.make_async_copy(adj.at[part], a_v.at[part], adj_sem.at[k])

    for k in range(ADJ_FIRST):
        adj_copy(k).start()
    a_v[slots] = jnp.zeros((tile, tile), BF16)

    hw = feat.shape[1] // 2

    def x_piece(i, h):
        r = 2 * chip_at(i) + core
        return x_v.at[h, pl.ds(pl.multiple_of(r * piece, piece), piece)]

    for h in range(2):
        x_v[h, pl.ds(pl.multiple_of(row * piece, piece), piece), :] = feat[:, h * hw : (h + 1) * hw]

    barrier = pltpu.get_barrier_semaphore()
    for i in range(1, n_row):
        pl.semaphore_signal(barrier, inc=1, device_id=((row + i) % n_row, col), device_id_type=MESH)
    for i in range(1, n_col):
        pl.semaphore_signal(barrier, inc=1, device_id=(row, (col + i) % n_col), device_id_type=MESH)
    pl.semaphore_wait(barrier, n_row + n_col - 2)

    def x_relay(i, h):
        n = chips * h + i
        return remote(x_piece(i, h), x_piece(i, h), xr_send.at[n], xr_recv.at[n], (partner, col))

    def merge(k, carry):
        s = slots - 1 - k
        a_v[s] = a_v[s] + a_v[next_of[s]]
        return carry

    x_step0, x_step1, x_finish = gather(
        x_piece, row_device, half_r, x_send, x_recv, lambda i, h: x_relay(i, h).start()
    )
    x_step0(0)
    x_step1(0)
    x_relay(0, 0).start()
    x_relay(0, 1).start()
    for k in range(ADJ_FIRST, ADJ_CHUNKS):
        adj_copy(k).start()
    x_step0(2)
    x_step0(3)
    x_step0(1)
    x_step1(2)
    for k in range(ADJ_CHUNKS):
        adj_copy(k).wait()
    lax.fori_loop(0, slots // 2, merge, 0)
    x_step1(3)
    x_step1(1)
    lax.fori_loop(slots // 2, slots, merge, 0)
    x_step0(4)
    for i in range(chips):
        x_relay(i, 0).wait_recv()

    def forward(mine, h):
        dest = col_at(mine)
        parts = []
        for t in range(per):
            base = (dest * per + t) * col_tiles
            parts.append(jnp.concatenate([a_v[slot_of[base + k]] for k in range(col_tiles)], axis=1))
        acc2[h, mine] = jnp.dot(jnp.concatenate(parts, axis=0), x_v[h], preferred_element_type=F32)

    s2_step, s2_finish = scatter(
        lambda i, h: acc2[h, i], col_device, half_c, send2, recv2, s2_send, s2_recv
    )

    def x_end():
        for i in range(chips):
            x_relay(i, 1).wait_recv()

    def do(step, *which):
        return lambda: [step(k, h) for k, h in which] and None

    run_steps(first_steps, half_c, forward, {
        0: do(s2_step, (0, 0)),
        1: lambda: (s2_step(1, 0), x_step1(4)) and None,
        2: do(s2_step, (2, 0)),
        3: do(s2_step, (3, 0)),
        4: lambda: (s2_step(4, 0), x_end()) and None,
        5: do(s2_step, (0, 1)),
        6: do(s2_step, (1, 1)),
        7: do(s2_step, (2, 1)),
    })
    run_steps(second_steps, half_c, forward, {
        0: do(s2_step, (5, 0)),
        1: do(s2_step, (6, 0)),
        2: do(s2_step, (3, 1)),
        3: do(s2_step, (4, 1)),
        4: do(s2_step, (5, 1)),
        5: do(s2_step, (6, 1)),
    })
    aggregated = jnp.concatenate([s2_step(7, 0), s2_step(7, 1)], axis=1).astype(BF16)

    pre = jnp.dot(aggregated, weight[...], preferred_element_type=F32)
    gate = jax.nn.sigmoid(pre)
    pre_grad = (upstream[...].astype(F32) * gate * (1.0 + pre * (1.0 - gate))).astype(BF16)
    grad_t = lax.dot_general(weight[...], pre_grad, (((1,), (1,)), ((), ())), preferred_element_type=F32)
    d_v[col] = grad_t.astype(BF16)

    def w1_copy(i):
        r = (row + i) % n_row
        return remote(wl.at[r], w1.at[i], w1_send.at[i], w1_recv.at[i], (r, col))

    def w2_copy(i):
        return remote(w2.at[col], w2.at[col], w2_send.at[i], w2_recv.at[i], (row, col_at(i)))

    def w3_copy(i):
        r = 2 * chip_at(i) + core
        return remote(w3.at[row], w3.at[row], w3_send.at[i], w3_recv.at[i], (r, col))

    def w3_relay(i):
        r = 2 * chip_at((half_r - i % half_r) % half_r + half_r * (i // half_r)) + core
        return remote(w3.at[r], w3.at[r], w3_send.at[chips + i], w3_recv.at[chips + i], (partner, col))

    def sum_slices():
        total = wl[row]
        for i in range(1, n_row):
            w1_copy(i).wait_recv()
            total = total + w1[i]
        w2[col] = total
        for i in range(1, n_col):
            w2_copy(i).start()

    d_step0, d_step1, d_finish = gather(
        lambda i, h: d_v.at[col_at(i), pl.ds(h * hw, hw)], col_device, half_c, d_send, d_recv, lambda i, h: None
    )
    d_step0(0)
    d_step1(0)
    hidden[...] = (pre * gate).astype(BF16)
    agg_t = jnp.transpose(aggregated.astype(F32)).astype(BF16)
    wl[...] = jnp.dot(agg_t, pre_grad, preferred_element_type=F32).reshape(wl.shape)
    for i in range(1, n_row):
        w1_copy(i).start()
    d_step0(2)
    d_step0(3)
    d_step0(1)
    d_step1(2)
    d_step1(3)
    d_step1(1)
    sum_slices()
    d_step0(4)

    def collect_slices():
        for i in range(1, n_col):
            w2_copy(i).wait_recv()
        slice_sum = w2[0]
        for c in range(1, n_col):
            slice_sum = slice_sum + w2[c]
        w3[row] = slice_sum * scale
        for i in range(1, chips):
            w3_copy(i).start()
        w3_relay(0).start()

    def transposed_part(dest, h):
        total = None
        for c in range(n_col):
            lines = []
            for t in range(per):
                base = (c * per + t) * col_tiles + dest * per
                lines.append(jnp.concatenate([a_v[slot_of[base + k]] for k in range(per)], axis=1))
            grad = d_v[c, pl.ds(pl.multiple_of(h * hw, hw), hw), :]
            part = jnp.dot(grad, jnp.concatenate(lines, axis=0), preferred_element_type=F32)
            total = part if total is None else total + part
        return total

    def p_copy(i, h):
        n = chips * h + i
        return remote(send_p.at[n], recv_p.at[n], p_send.at[n], p_recv.at[n], (partner, col))

    def backward(mine, h):
        send_p[chips * h + mine] = transposed_part(2 * chip_at(mine) + 1 - core, h).astype(BF16)
        p_copy(mine, h).start()
        acc4[h, mine] = transposed_part(2 * chip_at(mine) + core, h)

    def joint(i, h):
        p_copy(i, h).wait_recv()
        return acc4[h, i] + recv_p[chips * h + i].astype(F32)

    s4_step, s4_finish = scatter(joint, row_device, half_r, send4, recv4, s4_send, s4_recv)
    run_steps(first_steps, half_r, backward, {
        1: do(s4_step, (0, 0)),
        2: do(s4_step, (1, 0)),
        3: lambda: (s4_step(2, 0), d_step1(4)) and None,
        4: do(s4_step, (3, 0)),
        5: do(s4_step, (4, 0)),
        6: lambda: (s4_step(0, 1), collect_slices()) and None,
        7: do(s4_step, (1, 1)),
    })
    run_steps(second_steps, half_r, backward, {
        0: do(s4_step, (2, 1)),
        1: do(s4_step, (5, 0)),
        2: do(s4_step, (6, 0)),
        3: do(s4_step, (3, 1)),
        4: do(s4_step, (4, 1)),
        5: do(s4_step, (5, 1)),
        6: do(s4_step, (6, 1)),
    })
    for i in range(1, chips):
        w3_copy(i).wait_recv()
        w3_relay(i).start()
    for i in range(chips):
        w3_relay(i).wait_recv()
    weight_grad[...] = w3[...].reshape(weight_grad.shape)
    total = jnp.concatenate([s4_step(7, 0), s4_step(7, 1)], axis=0)
    feature_grad[...] = jnp.transpose(total).astype(BF16)

    x_finish()
    d_finish()
    s2_finish()
    s4_finish()
    for i in range(chips):
        for h in range(2):
            x_relay(i, h).wait_send()
            p_copy(i, h).wait_send()
        w3_relay(i).wait_send()
    for i in range(1, chips):
        w3_copy(i).wait_send()
    for i in range(1, n_col):
        w2_copy(i).wait_send()
    for i in range(1, n_row):
        w1_copy(i).wait_send()


def solution(mesh):
    n_row, n_col = mesh.shape["row"], mesh.shape["col"]
    chips = n_row // 2

    def shards(adj_tiles, tile_counts, tile_cols, features, weight, upstream):
        adj = adj_tiles[0, 0]
        slots, tile = adj.shape[0], adj.shape[1]
        piece, width = features.shape
        nodes = piece * n_row * n_col
        slot_of, next_of = slot_tables(tile_counts[0, 0], tile_cols[0, 0], piece * n_row // tile)
        sl = width // n_row
        dma = pltpu.SemaphoreType.DMA
        vmem = pl.BlockSpec(memory_space=pltpu.VMEM)
        smem = pl.BlockSpec(memory_space=pltpu.SMEM)
        out_shape = (
            jax.ShapeDtypeStruct((piece, width), BF16),
            jax.ShapeDtypeStruct((width, width), F32),
            jax.ShapeDtypeStruct((piece, width), BF16),
        )
        results = pl.pallas_call(
            functools.partial(layer_kernel, n_row, n_col, 1.0 / math.sqrt(nodes)),
            out_shape=out_shape,
            in_specs=[smem, smem, pl.BlockSpec(memory_space=pl.ANY), vmem, vmem, vmem],
            out_specs=(vmem, vmem, vmem),
            scratch_shapes=[
                pltpu.VMEM((slots + 1, tile, tile), BF16),
                pltpu.VMEM((2, piece * n_row, width // 2), BF16),
                pltpu.VMEM((n_col, width, piece), BF16),
                pltpu.VMEM((2, 8, piece, width // 2), F32),
                pltpu.VMEM((2, 8, width // 2, piece), F32),
                pltpu.VMEM((14, piece, width // 2), BF16), pltpu.VMEM((14, piece, width // 2), BF16),
                pltpu.VMEM((14, width // 2, piece), BF16), pltpu.VMEM((14, width // 2, piece), BF16),
                pltpu.VMEM((n_row, width // 2, piece), BF16), pltpu.VMEM((n_row, width // 2, piece), BF16),
                pltpu.VMEM((n_row, sl, width), F32),
                pltpu.VMEM((n_row, sl, width), F32),
                pltpu.VMEM((n_col, sl, width), F32),
                pltpu.VMEM((n_row, sl, width), F32),
                dma((ADJ_CHUNKS,)),
                dma((14,)), dma((14,)), dma((n_row,)), dma((n_row,)),
                dma((14,)), dma((14,)), dma((14,)), dma((14,)), dma((14,)), dma((14,)),
                dma((n_row,)), dma((n_row,)),
                dma((n_row,)), dma((n_row,)), dma((n_col,)), dma((n_col,)), dma((n_row,)), dma((n_row,)),
            ],
            compiler_params=pltpu.CompilerParams(
                collective_id=0, has_side_effects=True, vmem_limit_bytes=56 * 1024 * 1024
            ),
        )(slot_of, next_of, adj, features, weight, upstream)
        return pl.pallas_call(
            copy_kernel, out_shape=out_shape, in_specs=[vmem] * 3, out_specs=(vmem,) * 3
        )(*results)

    return jax.shard_map(
        shards,
        mesh=mesh,
        in_specs=(
            P("row", "col", None, None, None),
            P("row", "col", None),
            P("row", "col", None),
            P(("col", "row"), None),
            P(),
            P(("row", "col"), None),
        ),
        out_specs=(P(("row", "col"), None), P(), P(("col", "row"), None)),
        check_vma=False,
    )
```

```python
import functools
import math

import jax
import jax.numpy as jnp
from jax import lax
from jax.experimental import pallas as pl
from jax.experimental.pallas import tpu as pltpu
from jax.sharding import PartitionSpec as P

MESH = pl.DeviceIdType.MESH
F32, BF16 = jnp.float32, jnp.bfloat16
ADJ_CHUNKS = 8
ADJ_FIRST = 0


def table_kernel(counts, cols, slot_of, next_of):
    rows_t, slots = counts.shape[0], cols.shape[1]
    places = slot_of.shape[1]
    col_tiles = places // rows_t
    position = lax.broadcasted_iota(jnp.int32, (8, slots), 1)
    tile_row = jnp.zeros((8, slots), jnp.int32)
    ending = jnp.int32(0)
    for t in range(rows_t):
        ending = ending + counts[t]
        tile_row = tile_row + (position >= ending).astype(jnp.int32)
    ids = jnp.broadcast_to(cols[...], (8, slots))
    key = jnp.where(tile_row < rows_t, tile_row * col_tiles + ids, -1 - position)
    column = jnp.transpose(key)[:, 0:1]
    slot = lax.broadcasted_iota(jnp.int32, (slots, places), 0)
    place = lax.broadcasted_iota(jnp.int32, (slots, places), 1)
    slot_of[...] = jnp.min(jnp.where(column == place, slot, slots), axis=0, keepdims=True)
    slot = lax.broadcasted_iota(jnp.int32, (slots, slots), 0)
    other = lax.broadcasted_iota(jnp.int32, (slots, slots), 1)
    later = (column == key[0:1]) & (slot > other)
    next_of[...] = jnp.min(jnp.where(later, slot, slots), axis=0, keepdims=True)


def copy_kernel(*refs):
    for source, target in zip(refs[: len(refs) // 2], refs[len(refs) // 2 :]):
        target[...] = source[...]


def layer_kernel(
    n_row, n_col, scale,
    slot_of, next_of, adj, feat, weight, upstream,
    hidden, weight_grad, feature_grad,
    a_v, x_v, d_v, acc2, acc4, send2, recv2, send4, recv4, send_p, recv_p, wl, w1, w2, w3,
    adj_sem, x_send, x_recv, xr_send, xr_recv, d_send, d_recv, s2_send, s2_recv, s4_send, s4_recv,
    p_send, p_recv, w1_send, w1_recv, w2_send, w2_recv, w3_send, w3_recv,
):
    slots, tile = adj.shape[0], adj.shape[1]
    piece = feat.shape[0]
    per = piece // tile
    chips = n_row // 2
    col_tiles = per * n_row
    row = lax.axis_index("row")
    col = lax.axis_index("col")
    chip, core = row // 2, row % 2
    partner = row + 1 - 2 * core
    half_r, half_c = chips // 2, n_col // 2

    def chip_at(i):
        return ((chip // half_r + i // half_r) % 2) * half_r + (chip % half_r + i) % half_r

    def col_at(i):
        return ((col // half_c + i // half_c) % 2) * half_c + (col % half_c + i) % half_c

    def row_device(i):
        return 2 * chip_at(i) + core, col

    def col_device(i):
        return row, col_at(i)

    def remote(src, dst, send, recv, device):
        return pltpu.make_async_remote_copy(
            src_ref=src, dst_ref=dst, send_sem=send, recv_sem=recv, device_id=device, device_id_type=MESH
        )

    def gather(piece_at, device_at, half, send, recv, hook):
        moves = (
            (0, 1), (0, half - 1), (0, half),
            (0, 2),
            (half, 1), (half, half - 1),
            (2, half),
        )

        def make(h):
            up, down, plane, two, plane_up, plane_down, plane_two = [
                remote(piece_at(p, h), piece_at(p, h), send.at[7 * h + k], recv.at[7 * h + k], device_at(to))
                for k, (p, to) in enumerate(moves)
            ]

            def step(k):
                if k == 0:
                    two.start()
                    plane.start()
                    up.start()
                    down.start()
                elif k == 1:
                    up.wait_recv()
                    hook(half - 1, h)
                    down.wait_recv()
                    hook(1, h)
                elif k == 2:
                    plane.wait_recv()
                    plane_up.start()
                    plane_down.start()
                    hook(half, h)
                elif k == 3:
                    two.wait_recv()
                    plane_two.start()
                    hook(2, h)
                else:
                    plane_up.wait_recv()
                    hook(2 * half - 1, h)
                    plane_down.wait_recv()
                    hook(half + 1, h)
                    plane_two.wait_recv()
                    hook(half + 2, h)

            def finish():
                for copy in (up, down, plane, two, plane_up, plane_down, plane_two):
                    copy.wait_send()

            return step, finish

        (step0, finish0), (step1, finish1) = make(0), make(1)
        return step0, step1, lambda: (finish0(), finish1())

    def scatter(value_at, device_at, half, send_buf, recv_buf, send, recv):
        targets = (half, 1, half - 1, 1, half - 1, 2, half)
        offsets = (half + 2, half + 1, 2 * half - 1, 1, half - 1, 2, half, 0)

        def copy_of(k, h):
            n = 7 * h + k
            return remote(send_buf.at[n], recv_buf.at[n], send.at[n], recv.at[n], device_at(targets[k]))

        def got(k, h):
            copy_of(k, h).wait_recv()
            return recv_buf[7 * h + k].astype(F32)

        before = {5: (0,), 6: (1, 2), 7: (3, 4, 6, 5)}

        def step(k, h):
            value = value_at(offsets[k], h)
            for j in before.get(k, ()):
                value = value + got(j, h)
            if k < 7:
                send_buf[7 * h + k] = value.astype(BF16)
                copy_of(k, h).start()
            return value

        def finish():
            for h in range(2):
                for k in range(7):
                    copy_of(k, h).wait_send()

        return step, finish

    def packed(numbers):
        return sum(number * 8**k for k, number in enumerate(numbers))

    first_steps = ((0, 0), (1, 0), (2, 0), (3, 0), (4, 0), (0, 1), (1, 1), (2, 1))
    second_steps = ((3, 1), (5, 0), (4, 1), (6, 0), (5, 1), (6, 1), (7, 0), (7, 1))

    def run_steps(steps, half, compute, after):
        def body(n, codes):
            code, halves = codes
            compute(code % 8, halves % 8)
            for at, act in after.items():
                pl.when(n == at)(act)
            return code // 8, halves // 8

        offsets = (half + 2, half + 1, 2 * half - 1, 1, half - 1, 2, half, 0)
        lax.fori_loop(0, 8, body, (packed(offsets[k] for k, h in steps), packed(h for k, h in steps)))

    chunk = slots // ADJ_CHUNKS

    def adj_copy(k):
        part = pl.ds(k * chunk, chunk)
        return pltpu.make_async_copy(adj.at[part], a_v.at[part], adj_sem.at[k])

    for k in range(ADJ_FIRST):
        adj_copy(k).start()
    a_v[slots] = jnp.zeros((tile, tile), BF16)

    hw = feat.shape[1] // 2

    def x_piece(i, h):
        r = 2 * chip_at(i) + core
        return x_v.at[h, pl.ds(pl.multiple_of(r * piece, piece), piece)]

    for h in range(2):
        x_v[h, pl.ds(pl.multiple_of(row * piece, piece), piece), :] = feat[:, h * hw : (h + 1) * hw]

    barrier = pltpu.get_barrier_semaphore()
    for i in range(1, n_row):
        pl.semaphore_signal(barrier, inc=1, device_id=((row + i) % n_row, col), device_id_type=MESH)
    for i in range(1, n_col):
        pl.semaphore_signal(barrier, inc=1, device_id=(row, (col + i) % n_col), device_id_type=MESH)
    pl.semaphore_wait(barrier, n_row + n_col - 2)

    def x_relay(i, h):
        n = chips * h + i
        return remote(x_piece(i, h), x_piece(i, h), xr_send.at[n], xr_recv.at[n], (partner, col))

    def merge(k, carry):
        s = slots - 1 - k
        a_v[s] = a_v[s] + a_v[next_of[0, s]]
        return carry

    x_step0, x_step1, x_finish = gather(
        x_piece, row_device, half_r, x_send, x_recv, lambda i, h: x_relay(i, h).start()
    )
    x_step0(0)
    x_step1(0)
    x_relay(0, 0).start()
    x_relay(0, 1).start()
    for k in range(ADJ_FIRST, ADJ_CHUNKS):
        adj_copy(k).start()
    x_step0(2)
    x_step0(3)
    x_step0(1)
    x_step1(2)
    for k in range(ADJ_CHUNKS):
        adj_copy(k).wait()
    lax.fori_loop(0, slots // 2, merge, 0)
    x_step1(3)
    x_step1(1)
    lax.fori_loop(slots // 2, slots, merge, 0)
    x_step0(4)
    for i in range(chips):
        x_relay(i, 0).wait_recv()

    def forward(mine, h):
        dest = col_at(mine)
        parts = []
        for t in range(per):
            base = (dest * per + t) * col_tiles
            parts.append(jnp.concatenate([a_v[slot_of[0, base + k]] for k in range(col_tiles)], axis=1))
        acc2[h, mine] = jnp.dot(jnp.concatenate(parts, axis=0), x_v[h], preferred_element_type=F32)

    s2_step, s2_finish = scatter(
        lambda i, h: acc2[h, i], col_device, half_c, send2, recv2, s2_send, s2_recv
    )

    def x_end():
        for i in range(chips):
            x_relay(i, 1).wait_recv()

    def do(step, *which):
        return lambda: [step(k, h) for k, h in which] and None

    run_steps(first_steps, half_c, forward, {
        0: do(s2_step, (0, 0)),
        1: lambda: (s2_step(1, 0), x_step1(4)) and None,
        2: do(s2_step, (2, 0)),
        3: do(s2_step, (3, 0)),
        4: lambda: (s2_step(4, 0), x_end()) and None,
        5: do(s2_step, (0, 1)),
        6: do(s2_step, (1, 1)),
        7: do(s2_step, (2, 1)),
    })
    run_steps(second_steps, half_c, forward, {
        0: do(s2_step, (3, 1)),
        1: do(s2_step, (5, 0)),
        2: do(s2_step, (4, 1)),
        3: do(s2_step, (6, 0)),
        4: do(s2_step, (5, 1)),
        5: do(s2_step, (6, 1)),
    })
    aggregated = jnp.concatenate([s2_step(7, 0), s2_step(7, 1)], axis=1).astype(BF16)

    pre = jnp.dot(aggregated, weight[...], preferred_element_type=F32)
    gate = jax.nn.sigmoid(pre)
    pre_grad = (upstream[...].astype(F32) * gate * (1.0 + pre * (1.0 - gate))).astype(BF16)
    grad_t = lax.dot_general(weight[...], pre_grad, (((1,), (1,)), ((), ())), preferred_element_type=F32)
    d_v[col] = grad_t.astype(BF16)

    def w1_copy(i):
        r = (row + i) % n_row
        return remote(wl.at[r], w1.at[i], w1_send.at[i], w1_recv.at[i], (r, col))

    def w2_copy(i):
        return remote(w2.at[col], w2.at[col], w2_send.at[i], w2_recv.at[i], (row, col_at(i)))

    def w3_copy(i):
        r = 2 * chip_at(i) + core
        return remote(w3.at[row], w3.at[row], w3_send.at[i], w3_recv.at[i], (r, col))

    def w3_relay(i):
        r = 2 * chip_at((half_r - i % half_r) % half_r + half_r * (i // half_r)) + core
        return remote(w3.at[r], w3.at[r], w3_send.at[chips + i], w3_recv.at[chips + i], (partner, col))

    def sum_slices():
        total = wl[row]
        for i in range(1, n_row):
            w1_copy(i).wait_recv()
            total = total + w1[i]
        w2[col] = total
        for i in range(1, n_col):
            w2_copy(i).start()

    d_step0, d_step1, d_finish = gather(
        lambda i, h: d_v.at[col_at(i), pl.ds(h * hw, hw)], col_device, half_c, d_send, d_recv, lambda i, h: None
    )
    d_step0(0)
    d_step1(0)
    hidden[...] = (pre * gate).astype(BF16)
    agg_t = jnp.transpose(aggregated.astype(F32)).astype(BF16)
    wl[...] = jnp.dot(agg_t, pre_grad, preferred_element_type=F32).reshape(wl.shape)
    for i in range(1, n_row):
        w1_copy(i).start()
    d_step0(2)
    d_step0(3)
    d_step0(1)
    d_step1(2)
    d_step1(3)
    d_step1(1)
    sum_slices()
    d_step0(4)

    def collect_slices():
        for i in range(1, n_col):
            w2_copy(i).wait_recv()
        slice_sum = w2[0]
        for c in range(1, n_col):
            slice_sum = slice_sum + w2[c]
        w3[row] = slice_sum * scale
        for i in range(1, chips):
            w3_copy(i).start()
        w3_relay(0).start()

    def transposed_part(dest, h):
        total = None
        for c in range(n_col):
            lines = []
            for t in range(per):
                base = (c * per + t) * col_tiles + dest * per
                lines.append(jnp.concatenate([a_v[slot_of[0, base + k]] for k in range(per)], axis=1))
            grad = d_v[c, pl.ds(pl.multiple_of(h * hw, hw), hw), :]
            part = jnp.dot(grad, jnp.concatenate(lines, axis=0), preferred_element_type=F32)
            total = part if total is None else total + part
        return total

    def p_copy(i, h):
        n = chips * h + i
        return remote(send_p.at[n], recv_p.at[n], p_send.at[n], p_recv.at[n], (partner, col))

    def backward(mine, h):
        send_p[chips * h + mine] = transposed_part(2 * chip_at(mine) + 1 - core, h).astype(BF16)
        p_copy(mine, h).start()
        acc4[h, mine] = transposed_part(2 * chip_at(mine) + core, h)

    def joint(i, h):
        p_copy(i, h).wait_recv()
        return acc4[h, i] + recv_p[chips * h + i].astype(F32)

    s4_step, s4_finish = scatter(joint, row_device, half_r, send4, recv4, s4_send, s4_recv)
    run_steps(first_steps, half_r, backward, {
        1: do(s4_step, (0, 0)),
        2: do(s4_step, (1, 0)),
        3: lambda: (s4_step(2, 0), d_step1(4)) and None,
        4: do(s4_step, (3, 0)),
        5: do(s4_step, (4, 0)),
        6: lambda: (s4_step(0, 1), collect_slices()) and None,
        7: do(s4_step, (1, 1)),
    })
    run_steps(second_steps, half_r, backward, {
        0: do(s4_step, (2, 1)),
        1: do(s4_step, (3, 1)),
        2: do(s4_step, (5, 0)),
        3: do(s4_step, (4, 1)),
        4: do(s4_step, (6, 0)),
        5: do(s4_step, (5, 1)),
        6: do(s4_step, (6, 1)),
    })
    for i in range(1, chips):
        w3_copy(i).wait_recv()
        w3_relay(i).start()
    for i in range(chips):
        w3_relay(i).wait_recv()
    weight_grad[...] = w3[...].reshape(weight_grad.shape)
    for h in range(2):
        feature_grad[:, h * hw : (h + 1) * hw] = jnp.transpose(s4_step(7, h)).astype(BF16)

    x_finish()
    d_finish()
    s2_finish()
    s4_finish()
    for i in range(chips):
        for h in range(2):
            x_relay(i, h).wait_send()
            p_copy(i, h).wait_send()
        w3_relay(i).wait_send()
    for i in range(1, chips):
        w3_copy(i).wait_send()
    for i in range(1, n_col):
        w2_copy(i).wait_send()
    for i in range(1, n_row):
        w1_copy(i).wait_send()


def solution(mesh):
    n_row, n_col = mesh.shape["row"], mesh.shape["col"]
    chips = n_row // 2

    def shards(adj_tiles, tile_counts, tile_cols, features, weight, upstream):
        adj = adj_tiles[0, 0]
        slots, tile = adj.shape[0], adj.shape[1]
        piece, width = features.shape
        nodes = piece * n_row * n_col
        sl = width // n_row
        dma = pltpu.SemaphoreType.DMA
        vmem = pl.BlockSpec(memory_space=pltpu.VMEM)
        smem = pl.BlockSpec(memory_space=pltpu.SMEM)
        out_shape = (
            jax.ShapeDtypeStruct((piece, width), BF16),
            jax.ShapeDtypeStruct((width, width), F32),
            jax.ShapeDtypeStruct((piece, width), BF16),
        )
        rows_t = tile_counts.shape[2]
        slot_of, next_of = pl.pallas_call(
            table_kernel,
            out_shape=(
                jax.ShapeDtypeStruct((1, rows_t * (piece * n_row // tile)), jnp.int32),
                jax.ShapeDtypeStruct((1, slots), jnp.int32),
            ),
            in_specs=[smem, vmem],
            out_specs=(vmem, vmem),
        )(tile_counts[0, 0], tile_cols[0])
        results = pl.pallas_call(
            functools.partial(layer_kernel, n_row, n_col, 1.0 / math.sqrt(nodes)),
            out_shape=out_shape,
            in_specs=[smem, smem, pl.BlockSpec(memory_space=pl.ANY), vmem, vmem, vmem],
            out_specs=(vmem, vmem, vmem),
            scratch_shapes=[
                pltpu.VMEM((slots + 1, tile, tile), BF16),
                pltpu.VMEM((2, piece * n_row, width // 2), BF16),
                pltpu.VMEM((n_col, width, piece), BF16),
                pltpu.VMEM((2, 8, piece, width // 2), F32),
                pltpu.VMEM((2, 8, width // 2, piece), F32),
                pltpu.VMEM((14, piece, width // 2), BF16), pltpu.VMEM((14, piece, width // 2), BF16),
                pltpu.VMEM((14, width // 2, piece), BF16), pltpu.VMEM((14, width // 2, piece), BF16),
                pltpu.VMEM((n_row, width // 2, piece), BF16), pltpu.VMEM((n_row, width // 2, piece), BF16),
                pltpu.VMEM((n_row, sl, width), F32),
                pltpu.VMEM((n_row, sl, width), F32),
                pltpu.VMEM((n_col, sl, width), F32),
                pltpu.VMEM((n_row, sl, width), F32),
                dma((ADJ_CHUNKS,)),
                dma((14,)), dma((14,)), dma((n_row,)), dma((n_row,)),
                dma((14,)), dma((14,)), dma((14,)), dma((14,)), dma((14,)), dma((14,)),
                dma((n_row,)), dma((n_row,)),
                dma((n_row,)), dma((n_row,)), dma((n_col,)), dma((n_col,)), dma((n_row,)), dma((n_row,)),
            ],
            compiler_params=pltpu.CompilerParams(
                collective_id=0, has_side_effects=True, vmem_limit_bytes=56 * 1024 * 1024
            ),
        )(slot_of, next_of, adj, features, weight, upstream)
        return pl.pallas_call(
            copy_kernel, out_shape=out_shape, in_specs=[vmem] * 3, out_specs=(vmem,) * 3
        )(*results)

    return jax.shard_map(
        shards,
        mesh=mesh,
        in_specs=(
            P("row", "col", None, None, None),
            P("row", "col", None),
            P("row", "col", None),
            P(("col", "row"), None),
            P(),
            P(("row", "col"), None),
        ),
        out_specs=(P(("row", "col"), None), P(), P(("col", "row"), None)),
        check_vma=False,
    )
```

```python
import functools
import math

import jax
import jax.numpy as jnp
from jax import lax
from jax.experimental import pallas as pl
from jax.experimental.pallas import tpu as pltpu
from jax.sharding import PartitionSpec as P

MESH = pl.DeviceIdType.MESH
F32, BF16 = jnp.float32, jnp.bfloat16
ADJ_CHUNKS = 8
ADJ_FIRST = 0


def table_kernel(counts, cols, slot_of, next_of):
    rows_t, slots = counts.shape[0], cols.shape[1]
    places = slot_of.shape[1]
    col_tiles = places // rows_t
    position = lax.broadcasted_iota(jnp.int32, (8, slots), 1)
    tile_row = jnp.zeros((8, slots), jnp.int32)
    ending = jnp.int32(0)
    for t in range(rows_t):
        ending = ending + counts[t]
        tile_row = tile_row + (position >= ending).astype(jnp.int32)
    ids = jnp.broadcast_to(cols[...], (8, slots))
    key = jnp.where(tile_row < rows_t, tile_row * col_tiles + ids, -1 - position)
    column = jnp.transpose(key)[:, 0:1]
    slot = lax.broadcasted_iota(jnp.int32, (slots, places), 0)
    place = lax.broadcasted_iota(jnp.int32, (slots, places), 1)
    slot_of[...] = jnp.min(jnp.where(column == place, slot, slots), axis=0, keepdims=True)
    slot = lax.broadcasted_iota(jnp.int32, (slots, slots), 0)
    other = lax.broadcasted_iota(jnp.int32, (slots, slots), 1)
    later = (column == key[0:1]) & (slot > other)
    next_of[...] = jnp.min(jnp.where(later, slot, slots), axis=0, keepdims=True)


def copy_kernel(*refs):
    for source, target in zip(refs[: len(refs) // 2], refs[len(refs) // 2 :]):
        target[...] = source[...]


def layer_kernel(
    n_row, n_col, scale,
    slot_of, next_of, adj, feat, weight, upstream,
    hidden, weight_grad, feature_grad,
    a_v, x_v, d_v, acc2, acc4, send2, recv2, send4, recv4, send_p, recv_p, wl, w1, w2, w3,
    adj_sem, x_send, x_recv, xr_send, xr_recv, d_send, d_recv, s2_send, s2_recv, s4_send, s4_recv,
    p_send, p_recv, w1_send, w1_recv, w2_send, w2_recv, w3_send, w3_recv,
):
    slots, tile = adj.shape[0], adj.shape[1]
    piece = feat.shape[0]
    per = piece // tile
    chips = n_row // 2
    col_tiles = per * n_row
    row = lax.axis_index("row")
    col = lax.axis_index("col")
    chip, core = row // 2, row % 2
    partner = row + 1 - 2 * core
    half_r, half_c = chips // 2, n_col // 2

    barrier = pltpu.get_barrier_semaphore()
    for i in range(1, n_row):
        pl.semaphore_signal(barrier, inc=1, device_id=((row + i) % n_row, col), device_id_type=MESH)
    for i in range(1, n_col):
        pl.semaphore_signal(barrier, inc=1, device_id=(row, (col + i) % n_col), device_id_type=MESH)

    def chip_at(i):
        return ((chip // half_r + i // half_r) % 2) * half_r + (chip % half_r + i) % half_r

    def col_at(i):
        return ((col // half_c + i // half_c) % 2) * half_c + (col % half_c + i) % half_c

    def row_device(i):
        return 2 * chip_at(i) + core, col

    def col_device(i):
        return row, col_at(i)

    def remote(src, dst, send, recv, device):
        return pltpu.make_async_remote_copy(
            src_ref=src, dst_ref=dst, send_sem=send, recv_sem=recv, device_id=device, device_id_type=MESH
        )

    def gather(piece_at, device_at, half, send, recv, hook):
        moves = (
            (0, 1), (0, half - 1), (0, half),
            (0, 2),
            (half, 1), (half, half - 1),
            (2, half),
        )

        def make(h):
            up, down, plane, two, plane_up, plane_down, plane_two = [
                remote(piece_at(p, h), piece_at(p, h), send.at[7 * h + k], recv.at[7 * h + k], device_at(to))
                for k, (p, to) in enumerate(moves)
            ]

            def step(k):
                if k == 0:
                    two.start()
                    plane.start()
                    up.start()
                    down.start()
                elif k == 1:
                    up.wait_recv()
                    hook(half - 1, h)
                    down.wait_recv()
                    hook(1, h)
                elif k == 2:
                    plane.wait_recv()
                    plane_up.start()
                    plane_down.start()
                    hook(half, h)
                elif k == 3:
                    two.wait_recv()
                    plane_two.start()
                    hook(2, h)
                else:
                    plane_up.wait_recv()
                    hook(2 * half - 1, h)
                    plane_down.wait_recv()
                    hook(half + 1, h)
                    plane_two.wait_recv()
                    hook(half + 2, h)

            def finish():
                for copy in (up, down, plane, two, plane_up, plane_down, plane_two):
                    copy.wait_send()

            return step, finish

        (step0, finish0), (step1, finish1) = make(0), make(1)
        return step0, step1, lambda: (finish0(), finish1())

    def scatter(value_at, device_at, half, send_buf, recv_buf, send, recv):
        targets = (half, 1, half - 1, 1, half - 1, 2, half)
        offsets = (half + 2, half + 1, 2 * half - 1, 1, half - 1, 2, half, 0)

        def copy_of(k, h):
            n = 7 * h + k
            return remote(send_buf.at[n], recv_buf.at[n], send.at[n], recv.at[n], device_at(targets[k]))

        def got(k, h):
            copy_of(k, h).wait_recv()
            return recv_buf[7 * h + k].astype(F32)

        before = {5: (0,), 6: (1, 2), 7: (3, 4, 6, 5)}

        def step(k, h):
            value = value_at(offsets[k], h)
            for j in before.get(k, ()):
                value = value + got(j, h)
            if k < 7:
                send_buf[7 * h + k] = value.astype(BF16)
                copy_of(k, h).start()
            return value

        def finish():
            for h in range(2):
                for k in range(7):
                    copy_of(k, h).wait_send()

        return step, finish

    def packed(numbers):
        return sum(number * 8**k for k, number in enumerate(numbers))

    first_steps = ((0, 0), (1, 0), (2, 0), (3, 0), (4, 0), (0, 1), (1, 1), (2, 1))
    second_steps = ((3, 1), (5, 0), (4, 1), (6, 0), (5, 1), (6, 1), (7, 0), (7, 1))

    def run_steps(steps, half, compute, after):
        def body(n, codes):
            code, halves = codes
            compute(code % 8, halves % 8)
            for at, act in after.items():
                pl.when(n == at)(act)
            return code // 8, halves // 8

        offsets = (half + 2, half + 1, 2 * half - 1, 1, half - 1, 2, half, 0)
        lax.fori_loop(0, 8, body, (packed(offsets[k] for k, h in steps), packed(h for k, h in steps)))

    chunk = slots // ADJ_CHUNKS

    def adj_copy(k):
        part = pl.ds(k * chunk, chunk)
        return pltpu.make_async_copy(adj.at[part], a_v.at[part], adj_sem.at[k])

    for k in range(ADJ_FIRST):
        adj_copy(k).start()
    a_v[slots] = jnp.zeros((tile, tile), BF16)

    hw = feat.shape[1] // 2

    def x_piece(i, h):
        r = 2 * chip_at(i) + core
        return x_v.at[h, pl.ds(pl.multiple_of(r * piece, piece), piece)]

    for h in range(2):
        x_v[h, pl.ds(pl.multiple_of(row * piece, piece), piece), :] = feat[:, h * hw : (h + 1) * hw]

    pl.semaphore_wait(barrier, n_row + n_col - 2)

    def x_relay(i, h):
        n = chips * h + i
        return remote(x_piece(i, h), x_piece(i, h), xr_send.at[n], xr_recv.at[n], (partner, col))

    def merge(k, carry):
        s = slots - 1 - k
        a_v[s] = a_v[s] + a_v[next_of[0, s]]
        return carry

    x_step0, x_step1, x_finish = gather(
        x_piece, row_device, half_r, x_send, x_recv, lambda i, h: x_relay(i, h).start()
    )
    x_step0(0)
    x_step1(0)
    x_relay(0, 0).start()
    x_relay(0, 1).start()
    for k in range(ADJ_FIRST, ADJ_CHUNKS):
        adj_copy(k).start()
    x_step0(2)
    x_step0(3)
    x_step0(1)
    x_step1(2)
    for k in range(ADJ_CHUNKS):
        adj_copy(k).wait()
    lax.fori_loop(0, slots // 2, merge, 0)
    x_step1(3)
    x_step1(1)
    lax.fori_loop(slots // 2, slots, merge, 0)
    x_step0(4)
    for i in range(chips):
        x_relay(i, 0).wait_recv()

    def forward(mine, h):
        dest = col_at(mine)
        parts = []
        for t in range(per):
            base = (dest * per + t) * col_tiles
            parts.append(jnp.concatenate([a_v[slot_of[0, base + k]] for k in range(col_tiles)], axis=1))
        acc2[h, mine] = jnp.dot(jnp.concatenate(parts, axis=0), x_v[h], preferred_element_type=F32)

    s2_step, s2_finish = scatter(
        lambda i, h: acc2[h, i], col_device, half_c, send2, recv2, s2_send, s2_recv
    )

    def x_end():
        for i in range(chips):
            x_relay(i, 1).wait_recv()

    def do(step, *which):
        return lambda: [step(k, h) for k, h in which] and None

    run_steps(first_steps, half_c, forward, {
        0: do(s2_step, (0, 0)),
        1: lambda: (s2_step(1, 0), x_step1(4)) and None,
        2: do(s2_step, (2, 0)),
        3: do(s2_step, (3, 0)),
        4: lambda: (s2_step(4, 0), x_end()) and None,
        5: do(s2_step, (0, 1)),
        6: do(s2_step, (1, 1)),
        7: do(s2_step, (2, 1)),
    })
    run_steps(second_steps, half_c, forward, {
        0: do(s2_step, (3, 1)),
        1: do(s2_step, (5, 0)),
        2: do(s2_step, (4, 1)),
        3: do(s2_step, (6, 0)),
        4: do(s2_step, (5, 1)),
        5: do(s2_step, (6, 1)),
    })
    aggregated = jnp.concatenate([s2_step(7, 0), s2_step(7, 1)], axis=1).astype(BF16)

    pre = jnp.dot(aggregated, weight[...], preferred_element_type=F32)
    gate = jax.nn.sigmoid(pre)
    pre_grad = (upstream[...].astype(F32) * gate * (1.0 + pre * (1.0 - gate))).astype(BF16)
    grad_t = lax.dot_general(weight[...], pre_grad, (((1,), (1,)), ((), ())), preferred_element_type=F32)
    d_v[col] = grad_t.astype(BF16)

    def w1_copy(i):
        r = (row + i) % n_row
        return remote(wl.at[r], w1.at[i], w1_send.at[i], w1_recv.at[i], (r, col))

    def w2_copy(i):
        return remote(w2.at[col], w2.at[col], w2_send.at[i], w2_recv.at[i], (row, col_at(i)))

    def w3_copy(i):
        r = 2 * chip_at(i) + core
        return remote(w3.at[row], w3.at[row], w3_send.at[i], w3_recv.at[i], (r, col))

    def w3_relay(i):
        r = 2 * chip_at((half_r - i % half_r) % half_r + half_r * (i // half_r)) + core
        return remote(w3.at[r], w3.at[r], w3_send.at[chips + i], w3_recv.at[chips + i], (partner, col))

    def sum_slices():
        total = wl[row]
        for i in range(1, n_row):
            w1_copy(i).wait_recv()
            total = total + w1[i]
        w2[col] = total
        for i in range(1, n_col):
            w2_copy(i).start()

    d_step0, d_step1, d_finish = gather(
        lambda i, h: d_v.at[col_at(i), pl.ds(h * hw, hw)], col_device, half_c, d_send, d_recv, lambda i, h: None
    )
    d_step0(0)
    d_step1(0)
    hidden[...] = (pre * gate).astype(BF16)
    agg_t = jnp.transpose(aggregated.astype(F32)).astype(BF16)
    wl[...] = jnp.dot(agg_t, pre_grad, preferred_element_type=F32).reshape(wl.shape)
    for i in range(1, n_row):
        w1_copy(i).start()
    d_step0(2)
    d_step0(3)
    d_step0(1)
    d_step1(2)
    d_step1(3)
    d_step1(1)
    sum_slices()
    d_step0(4)

    def collect_slices():
        for i in range(1, n_col):
            w2_copy(i).wait_recv()
        slice_sum = w2[0]
        for c in range(1, n_col):
            slice_sum = slice_sum + w2[c]
        w3[row] = slice_sum * scale
        for i in range(1, chips):
            w3_copy(i).start()
        w3_relay(0).start()

    def transposed_part(dest, h):
        lines = []
        for c in range(n_col):
            for t in range(per):
                base = (c * per + t) * col_tiles + dest * per
                lines.append(jnp.concatenate([a_v[slot_of[0, base + k]] for k in range(per)], axis=1))
        rows = pl.ds(pl.multiple_of(h * hw, hw), hw)
        grads = jnp.concatenate([d_v[c, rows, :] for c in range(n_col)], axis=1)
        return jnp.dot(grads, jnp.concatenate(lines, axis=0), preferred_element_type=F32)

    def p_copy(i, h):
        n = chips * h + i
        return remote(send_p.at[n], recv_p.at[n], p_send.at[n], p_recv.at[n], (partner, col))

    def backward(mine, h):
        send_p[chips * h + mine] = transposed_part(2 * chip_at(mine) + 1 - core, h).astype(BF16)
        p_copy(mine, h).start()
        acc4[h, mine] = transposed_part(2 * chip_at(mine) + core, h)

    def joint(i, h):
        p_copy(i, h).wait_recv()
        return acc4[h, i] + recv_p[chips * h + i].astype(F32)

    s4_step, s4_finish = scatter(joint, row_device, half_r, send4, recv4, s4_send, s4_recv)
    run_steps(first_steps, half_r, backward, {
        1: do(s4_step, (0, 0)),
        2: do(s4_step, (1, 0)),
        3: lambda: (s4_step(2, 0), d_step1(4)) and None,
        4: do(s4_step, (3, 0)),
        5: do(s4_step, (4, 0)),
        6: lambda: (s4_step(0, 1), collect_slices()) and None,
        7: do(s4_step, (1, 1)),
    })
    run_steps(second_steps, half_r, backward, {
        0: do(s4_step, (2, 1)),
        1: do(s4_step, (3, 1)),
        2: do(s4_step, (5, 0)),
        3: do(s4_step, (4, 1)),
        4: do(s4_step, (6, 0)),
        5: do(s4_step, (5, 1)),
        6: do(s4_step, (6, 1)),
    })
    for i in range(1, chips):
        w3_copy(i).wait_recv()
        w3_relay(i).start()
    for i in range(chips):
        w3_relay(i).wait_recv()
    weight_grad[...] = w3[...].reshape(weight_grad.shape)
    for h in range(2):
        feature_grad[:, h * hw : (h + 1) * hw] = jnp.transpose(s4_step(7, h)).astype(BF16)

    x_finish()
    d_finish()
    s2_finish()
    s4_finish()
    for i in range(chips):
        for h in range(2):
            x_relay(i, h).wait_send()
            p_copy(i, h).wait_send()
        w3_relay(i).wait_send()
    for i in range(1, chips):
        w3_copy(i).wait_send()
    for i in range(1, n_col):
        w2_copy(i).wait_send()
    for i in range(1, n_row):
        w1_copy(i).wait_send()


def solution(mesh):
    n_row, n_col = mesh.shape["row"], mesh.shape["col"]
    chips = n_row // 2

    def shards(adj_tiles, tile_counts, tile_cols, features, weight, upstream):
        adj = adj_tiles[0, 0]
        slots, tile = adj.shape[0], adj.shape[1]
        piece, width = features.shape
        nodes = piece * n_row * n_col
        sl = width // n_row
        dma = pltpu.SemaphoreType.DMA
        vmem = pl.BlockSpec(memory_space=pltpu.VMEM)
        smem = pl.BlockSpec(memory_space=pltpu.SMEM)
        out_shape = (
            jax.ShapeDtypeStruct((piece, width), BF16),
            jax.ShapeDtypeStruct((width, width), F32),
            jax.ShapeDtypeStruct((piece, width), BF16),
        )
        rows_t = tile_counts.shape[2]
        slot_of, next_of = pl.pallas_call(
            table_kernel,
            out_shape=(
                jax.ShapeDtypeStruct((1, rows_t * (piece * n_row // tile)), jnp.int32),
                jax.ShapeDtypeStruct((1, slots), jnp.int32),
            ),
            in_specs=[smem, vmem],
            out_specs=(vmem, vmem),
        )(tile_counts[0, 0], tile_cols[0])
        results = pl.pallas_call(
            functools.partial(layer_kernel, n_row, n_col, 1.0 / math.sqrt(nodes)),
            out_shape=out_shape,
            in_specs=[smem, smem, pl.BlockSpec(memory_space=pl.ANY), vmem, vmem, vmem],
            out_specs=(vmem, vmem, vmem),
            scratch_shapes=[
                pltpu.VMEM((slots + 1, tile, tile), BF16),
                pltpu.VMEM((2, piece * n_row, width // 2), BF16),
                pltpu.VMEM((n_col, width, piece), BF16),
                pltpu.VMEM((2, 8, piece, width // 2), F32),
                pltpu.VMEM((2, 8, width // 2, piece), F32),
                pltpu.VMEM((14, piece, width // 2), BF16), pltpu.VMEM((14, piece, width // 2), BF16),
                pltpu.VMEM((14, width // 2, piece), BF16), pltpu.VMEM((14, width // 2, piece), BF16),
                pltpu.VMEM((n_row, width // 2, piece), BF16), pltpu.VMEM((n_row, width // 2, piece), BF16),
                pltpu.VMEM((n_row, sl, width), F32),
                pltpu.VMEM((n_row, sl, width), F32),
                pltpu.VMEM((n_col, sl, width), F32),
                pltpu.VMEM((n_row, sl, width), F32),
                dma((ADJ_CHUNKS,)),
                dma((14,)), dma((14,)), dma((n_row,)), dma((n_row,)),
                dma((14,)), dma((14,)), dma((14,)), dma((14,)), dma((14,)), dma((14,)),
                dma((n_row,)), dma((n_row,)),
                dma((n_row,)), dma((n_row,)), dma((n_col,)), dma((n_col,)), dma((n_row,)), dma((n_row,)),
            ],
            compiler_params=pltpu.CompilerParams(
                collective_id=0, has_side_effects=True, vmem_limit_bytes=56 * 1024 * 1024
            ),
        )(slot_of, next_of, adj, features, weight, upstream)
        return pl.pallas_call(
            copy_kernel, out_shape=out_shape, in_specs=[vmem] * 3, out_specs=(vmem,) * 3
        )(*results)

    return jax.shard_map(
        shards,
        mesh=mesh,
        in_specs=(
            P("row", "col", None, None, None),
            P("row", "col", None),
            P("row", "col", None),
            P(("col", "row"), None),
            P(),
            P(("row", "col"), None),
        ),
        out_specs=(P(("row", "col"), None), P(), P(("col", "row"), None)),
        check_vma=False,
    )
```
